512 devices in a mesh: docs: 128 (over y, z, core), split: 4 (over x).
Axes of the slice: x: 4, y: 8, z: 8, core: 2. Of those that a mesh axis runs over, the one named last changes fastest.
Arguments:
- embeddings: bfloat16 [65536, 1024], P(('docs', 'split')), may hold values from -480 to 480
- cluster_id: int32 [65536], P(('docs', 'split')), may hold values from 0 to 255, as said below
- rank: int32 [65536], P(('docs', 'split')), may hold values from 0 to 65535, each once
Outputs:
- dup_score: float32 [65536], P(('docs', 'split'))
The draws below stay inside these ranges and needn't reach their ends.
Inputs may be any that keep to these rules, and one draw needn't show every extreme that they name: `cluster_id`: cluster c belongs to owner c // 2. In each aligned block of 128 documents (the documents of one device) at most 2 documents belong to any one owner, and one owner receives exactly 2 from every block.
All inputs are finite; a program needn't handle non-finite values.
Results may differ from the reference program's by a relative error of at most 0.00056.
Values may be sent and summed in bfloat16 or wider, within the bound.
No kernel may reach another device: no remote copies, remote signals or barrier semaphores. Data moves between devices by JAX's collectives and lax.ppermute only.
A program may use at most 64 MiB of HBM per device.

```python
import math
import jax
import jax.numpy as jnp
from jax import lax

D = 1024
DOC_DEV = 128
CL_DEV = 2
CLUSTERS = 256
NDOC = 65536
OWNER_MAX = 1024


def doc_clusters(key):
    base_key = jax.random.fold_in(key, 7)
    owners = CLUSTERS // CL_DEV
    blocks = NDOC // DOC_DEV
    base_count = DOC_DEV // owners
    key_hot, key_low, key_blocks = jax.random.split(base_key, 3)
    hot = jax.random.randint(key_hot, (), 0, owners)
    low_shift = jax.random.randint(key_low, (owners,), 0, base_count + 1)
    block_keys = jax.random.split(key_blocks, blocks)

    def one_block(block_key):
        key_order, key_shift, key_shuffle, key_within = jax.random.split(block_key, 4)
        shuffled = jax.random.permutation(key_order, owners)
        shuffled = jnp.where(shuffled == hot, shuffled[0], shuffled).at[0].set(hot)
        firsts = shuffled[0::2]
        seconds = shuffled[1::2]
        drawn = jax.random.randint(key_shift, (owners // 2,), 0, 1 << 20)
        lower = low_shift[firsts]
        shift = lower + drawn % (base_count + 1 - lower)
        shift = shift.at[0].set(base_count)
        counts = jnp.zeros((owners,), jnp.int32).at[firsts].set(base_count + shift).at[seconds].set(base_count - shift)
        ends = jnp.cumsum(counts)
        position = jnp.arange(DOC_DEV, dtype=jnp.int32)
        owner_at = jnp.searchsorted(ends, position, side='right').astype(jnp.int32)
        owner_at = jax.random.permutation(key_shuffle, owner_at)
        within = jax.random.randint(key_within, (DOC_DEV,), 0, CL_DEV)
        return owner_at * CL_DEV + within
    return jax.vmap(one_block)(block_keys).reshape(-1).astype(jnp.int32)


def draw_cluster_id(key, part):
    return doc_clusters(key)


def draw_embeddings(key, part):
    clusters = doc_clusters(key)
    topics = 48
    key_center, key_topic, key_pick, key_noise, key_scale, key_column, key_row = jax.random.split(jax.random.fold_in(key, 11), 7)
    centers = jax.random.truncated_normal(key_center, -4.0, 4.0, (CLUSTERS, D), jnp.float32)
    topic_rows = jax.random.truncated_normal(key_topic, -4.0, 4.0, (CLUSTERS * topics, D), jnp.float32)
    topic_id = clusters * topics + jax.random.randint(key_pick, (NDOC,), 0, topics)
    column_scale = jnp.exp(jax.random.uniform(key_column, (1, D), jnp.float32, math.log(0.3), math.log(3.0)))
    row_scale = jnp.exp(jax.random.uniform(key_row, (NDOC, 1), jnp.float32, 0.0, math.log(10.0)))
    noise = jax.random.truncated_normal(key_noise, -4.0, 4.0, (NDOC, D), jnp.float32)
    spread = jnp.exp(jax.random.uniform(key_scale, (NDOC, 1), jnp.float32, math.log(0.2), math.log(2.0)))
    values = (centers[clusters] + topic_rows[topic_id] + spread * noise) * column_scale * row_scale
    return values.astype(jnp.bfloat16)


def setup_inputs(seed: int = 0) -> dict:
    keys = jax.random.split(jax.random.key(seed), 4)
    embeddings = draw_embeddings(jax.random.fold_in(keys[3], 71), 0)
    cluster_id = draw_cluster_id(jax.random.fold_in(keys[3], 71), 0)
    rank = jax.random.permutation(keys[2], NDOC).astype(jnp.int32)
    return {"embeddings": embeddings, "cluster_id": cluster_id, "rank": rank}


EPSILON = 1e-06

def reference(embeddings, cluster_id, rank):
    values = embeddings.astype(jnp.float32)
    unit = (values / jnp.sqrt(lax.optimization_barrier(jnp.sum(values * values, axis=1, keepdims=True)) + EPSILON)).astype(jnp.bfloat16)
    owners = CLUSTERS // CL_DEV
    owner = (cluster_id // CL_DEV).astype(jnp.int32)
    order = jnp.argsort(owner, stable=True).astype(jnp.int32)
    counts = jax.ops.segment_sum(jnp.ones((NDOC,), jnp.int32), owner, owners).astype(jnp.int32)
    offsets = (jnp.cumsum(counts) - counts).astype(jnp.int32)
    sorted_rows = jnp.concatenate([unit[order], jnp.zeros((OWNER_MAX, D), jnp.bfloat16)], axis=0)
    sorted_cluster = jnp.concatenate([cluster_id[order], jnp.full((OWNER_MAX,), -1, jnp.int32)]).astype(jnp.int32)
    sorted_rank = jnp.concatenate([rank[order], jnp.zeros((OWNER_MAX,), jnp.int32)]).astype(jnp.int32)

    def per_owner(first_row):
        rows_here = lax.dynamic_slice_in_dim(sorted_rows, first_row, OWNER_MAX, 0)
        cluster_here = lax.dynamic_slice_in_dim(sorted_cluster, first_row, OWNER_MAX, 0)
        rank_here = lax.dynamic_slice_in_dim(sorted_rank, first_row, OWNER_MAX, 0)
        gram = jnp.dot(rows_here, rows_here.T, preferred_element_type=jnp.float32)
        allowed = (cluster_here[:, None] == cluster_here[None, :]) & (rank_here[None, :] < rank_here[:, None])
        return lax.optimization_barrier(jnp.max(jnp.where(allowed, gram, -1.0), axis=1))
    top_scores = lax.map(per_owner, offsets)
    sorted_owner = owner[order]
    within = (jnp.arange(NDOC).astype(jnp.int32) - offsets[sorted_owner]).astype(jnp.int32)
    picked = top_scores[sorted_owner, within]
    return jnp.zeros((NDOC,), jnp.float32).at[order].set(picked)
```

```python
import jax
import jax.numpy as jnp
from jax import lax
from jax.experimental import pallas as pl
from jax.experimental.pallas import tpu as pltpu
from jax.sharding import PartitionSpec as P

EPSILON = 1e-06
SLOTS = 2
LANES = 128


def pack_kernel(rows_ref, cluster_ref, rank_ref, send_ref, place_ref):
    docs, width = rows_ref.shape
    slots = send_ref.shape[0]
    values = rows_ref[...].astype(jnp.float32)
    total = jnp.sum(values * values, axis=1, keepdims=True)
    unit = (values / jnp.sqrt(total + EPSILON)).astype(jnp.bfloat16)
    cluster = jnp.broadcast_to(cluster_ref[...], (docs, docs))
    rank = jnp.broadcast_to(rank_ref[...], (docs, docs))
    row = lax.broadcasted_iota(jnp.int32, (docs, docs), 0)
    col = lax.broadcasted_iota(jnp.int32, (docs, docs), 1)
    cluster_col = jnp.sum(jnp.where(row == col, cluster, 0), axis=1, keepdims=True)
    rank_col = jnp.sum(jnp.where(row == col, rank, 0), axis=1, keepdims=True)
    earlier = (cluster_col == cluster) & (row < col)
    slot = jnp.sum(earlier.astype(jnp.int32), axis=0, keepdims=True)
    place = cluster_ref[...] * SLOTS + slot
    place_ref[...] = place
    age = 65536 - rank_col
    high = age // 256
    low = age - high * 256
    lane = lax.broadcasted_iota(jnp.int32, (docs, LANES), 1)
    digits = jnp.where(lane == 0, high, jnp.where(lane == 1, low, 0))
    digits = digits.astype(jnp.float32).astype(jnp.bfloat16)
    target = lax.broadcasted_iota(jnp.int32, (slots, docs), 0)
    onehot = (target == jnp.broadcast_to(place, (slots, docs))).astype(jnp.float32).astype(jnp.bfloat16)
    send_ref[:, :width] = jnp.dot(onehot, unit, preferred_element_type=jnp.float32).astype(jnp.bfloat16)
    send_ref[:, width:] = jnp.dot(onehot, digits, preferred_element_type=jnp.float32).astype(jnp.bfloat16)


def ages(rows_ref, width):
    lane = lax.broadcasted_iota(jnp.int32, (LANES, LANES), 0)
    weight = jnp.where(lane == 0, 256.0, jnp.where(lane == 1, 1.0, 0.0)).astype(jnp.bfloat16)
    return weight, rows_ref[:, width:]


def best_of(keys_ref, queries_ref, width):
    weight, key_digits = ages(keys_ref, width)
    key_age = jnp.dot(key_digits, weight, preferred_element_type=jnp.float32)
    lane = lax.broadcasted_iota(jnp.int32, (8, LANES), 1)
    weight_row = jnp.where(lane == 0, 256.0, jnp.where(lane == 1, 1.0, 0.0)).astype(jnp.bfloat16)
    contract = (((1,), (1,)), ((), ()))
    query_age = lax.dot_general(weight_row, queries_ref[:, width:], contract, preferred_element_type=jnp.float32)
    count = queries_ref.shape[0]
    scores = lax.dot_general(keys_ref[:, :width], queries_ref[:, :width], contract, preferred_element_type=jnp.float32)
    allowed = key_age[:, :1] > query_age[:1, :]
    return jnp.max(jnp.where(allowed, scores, -1.0), axis=0, keepdims=True)


def make_own(width):
    def kernel(queries_ref, best_ref):
        best_ref[...] = best_of(queries_ref, queries_ref, width)

    return kernel


def make_peer(width):
    def kernel(queries_ref, keys_ref, best_ref, out_ref):
        best = jnp.maximum(best_ref[...], best_of(keys_ref, queries_ref, width))
        messages = out_ref.shape[0]
        count = best.shape[1]
        best = jnp.broadcast_to(best, (messages, count))
        row = lax.broadcasted_iota(jnp.int32, (messages, count), 0) * SLOTS
        col = lax.broadcasted_iota(jnp.int32, (messages, count), 1)
        first = jnp.sum(jnp.where(col == row, best, 0.0), axis=1, keepdims=True)
        second = jnp.sum(jnp.where(col == row + 1, best, 0.0), axis=1, keepdims=True)
        lane = lax.broadcasted_iota(jnp.int32, out_ref.shape, 1)
        out_ref[...] = jnp.where(lane == 0, first, second)

    return kernel


def unpack_kernel(scores_ref, place_ref, out_ref):
    clusters = scores_ref.shape[0]
    docs = place_ref.shape[1]
    place = jnp.broadcast_to(place_ref[...], (clusters, docs))
    row = lax.broadcasted_iota(jnp.int32, (clusters, docs), 0) * SLOTS
    first = jnp.where(place == row, scores_ref[:, 0:1], 0.0)
    second = jnp.where(place == row + 1, scores_ref[:, 1:2], 0.0)
    out_ref[...] = jnp.sum(first + second, axis=0, keepdims=True)


def make_per_device(docs_axis, split_axis):
    devices = docs_axis * split_axis
    clusters = devices // 2
    slots = clusters * SLOTS

    groups = [
        [d * split_axis + s for d in range(core, docs_axis, 2) for s in range(split_axis)]
        for core in range(2)
    ]
    partner = [(d, d ^ 1) for d in range(docs_axis)]
    both = ("docs", "split")

    def per_device(embeddings, cluster_id, rank):
        docs, width = embeddings.shape
        wide = width + LANES
        send, place = pl.pallas_call(
            pack_kernel,
            out_shape=(
                jax.ShapeDtypeStruct((slots, wide), jnp.bfloat16),
                jax.ShapeDtypeStruct((1, docs), jnp.int32),
            ),
            name="pack",
        )(embeddings, cluster_id.reshape(1, docs), rank.reshape(1, docs))
        got = lax.all_to_all(
            send.reshape(clusters, SLOTS, wide), both, 0, 0, axis_index_groups=groups, tiled=True
        )
        queries = got.reshape(slots, wide)
        keys = lax.ppermute(queries, "docs", partner)
        best = pl.pallas_call(
            make_own(width), out_shape=jax.ShapeDtypeStruct((1, slots), jnp.float32), name="own"
        )(queries)
        scores = pl.pallas_call(
            make_peer(width),
            out_shape=jax.ShapeDtypeStruct((clusters, LANES), jnp.float32),
            name="peer",
        )(queries, keys, best)
        back = lax.all_to_all(
            scores.reshape(clusters, 1, LANES), both, 0, 0, axis_index_groups=groups, tiled=True
        ).reshape(clusters, LANES)
        out = pl.pallas_call(
            unpack_kernel, out_shape=jax.ShapeDtypeStruct((1, docs), jnp.float32), name="unpack"
        )(back, place)
        return out.reshape(docs)

    return per_device


def solution(mesh):
    placed = (P(("docs", "split"), None), P(("docs", "split")), P(("docs", "split")))
    per_device = make_per_device(mesh.shape["docs"], mesh.shape["split"])
    return jax.shard_map(
        per_device, mesh=mesh, in_specs=placed, out_specs=P(("docs", "split")), check_vma=False
    )
```

```python
import jax
import jax.numpy as jnp
from jax import lax
from jax.experimental import pallas as pl
from jax.experimental.pallas import tpu as pltpu
from jax.sharding import PartitionSpec as P

EPSILON = 1e-06
SLOTS = 2
LANES = 128
PARAMS = pltpu.CompilerParams(vmem_limit_bytes=16 << 20)


def pack_kernel(rows_hbm, cluster_hbm, rank_hbm, send_ref, place_ref, rows_ref, cluster_ref, rank_ref, sems):
    load_cluster = pltpu.make_async_copy(cluster_hbm, cluster_ref, sems.at[0])
    load_rank = pltpu.make_async_copy(rank_hbm, rank_ref, sems.at[1])
    load_rows = pltpu.make_async_copy(rows_hbm, rows_ref, sems.at[2])
    load_cluster.start()
    load_rank.start()
    load_rows.start()
    docs, width = rows_ref.shape
    slots = send_ref.shape[0]
    row = lax.broadcasted_iota(jnp.int32, (docs, docs), 0)
    col = lax.broadcasted_iota(jnp.int32, (docs, docs), 1)
    lane = lax.broadcasted_iota(jnp.int32, (docs, LANES), 1)
    target = lax.broadcasted_iota(jnp.int32, (slots, docs), 0)
    load_cluster.wait()
    cluster = jnp.broadcast_to(cluster_ref[...], (docs, docs))
    cluster_col = jnp.sum(jnp.where(row == col, cluster, 0), axis=1, keepdims=True)
    earlier = (cluster_col == cluster) & (row < col)
    slot = jnp.sum(earlier.astype(jnp.int32), axis=0, keepdims=True)
    place = cluster_ref[...] * SLOTS + slot
    place_ref[...] = place
    onehot = (target == jnp.broadcast_to(place, (slots, docs))).astype(jnp.float32).astype(jnp.bfloat16)
    load_rank.wait()
    rank = jnp.broadcast_to(rank_ref[...], (docs, docs))
    age = 65536 - jnp.sum(jnp.where(row == col, rank, 0), axis=1, keepdims=True)
    high = age // 256
    low = age - high * 256
    digits = jnp.where(lane == 0, high, jnp.where(lane == 1, low, 0))
    digits = digits.astype(jnp.float32).astype(jnp.bfloat16)
    send_ref[:, width:] = jnp.dot(onehot, digits, preferred_element_type=jnp.float32).astype(jnp.bfloat16)
    load_rows.wait()
    values = rows_ref[...].astype(jnp.float32)
    total = jnp.sum(values * values, axis=1, keepdims=True)
    unit = (values / jnp.sqrt(total + EPSILON)).astype(jnp.bfloat16)
    send_ref[:, :width] = jnp.dot(onehot, unit, preferred_element_type=jnp.float32).astype(jnp.bfloat16)


def age_weights(shape, axis):
    place = lax.broadcasted_iota(jnp.int32, shape, axis)
    return jnp.where(place == 0, 256.0, jnp.where(place == 1, 1.0, 0.0)).astype(jnp.bfloat16)


def best_of(keys_ref, queries_ref, width):
    contract = (((1,), (1,)), ((), ()))
    key_age = jnp.dot(keys_ref[:, width:], age_weights((LANES, LANES), 0), preferred_element_type=jnp.float32)
    query_age = lax.dot_general(
        age_weights((8, LANES), 1), queries_ref[:, width:], contract, preferred_element_type=jnp.float32
    )
    scores = lax.dot_general(
        keys_ref[:, :width], queries_ref[:, :width], contract, preferred_element_type=jnp.float32
    )
    allowed = key_age[:, :1] > query_age[:1, :]
    return jnp.max(jnp.where(allowed, scores, -1.0), axis=0, keepdims=True)


def make_own(width):
    def kernel(queries_ref, best_ref):
        best_ref[...] = best_of(queries_ref, queries_ref, width)

    return kernel


def make_peer(width):
    def kernel(queries_ref, keys_ref, best_ref, out_ref):
        best = jnp.maximum(best_ref[...], best_of(keys_ref, queries_ref, width))
        messages = out_ref.shape[0]
        count = best.shape[1]
        best = jnp.broadcast_to(best, (messages, count))
        row = lax.broadcasted_iota(jnp.int32, (messages, count), 0) * SLOTS
        col = lax.broadcasted_iota(jnp.int32, (messages, count), 1)
        first = jnp.sum(jnp.where(col == row, best, 0.0), axis=1, keepdims=True)
        second = jnp.sum(jnp.where(col == row + 1, best, 0.0), axis=1, keepdims=True)
        lane = lax.broadcasted_iota(jnp.int32, out_ref.shape, 1)
        out_ref[...] = jnp.where(lane == 0, first, second)

    return kernel


def unpack_kernel(scores_ref, place_ref, out_ref):
    clusters = scores_ref.shape[0]
    docs = place_ref.shape[1]
    place = jnp.broadcast_to(place_ref[...], (clusters, docs))
    row = lax.broadcasted_iota(jnp.int32, (clusters, docs), 0) * SLOTS
    first = jnp.where(place == row, scores_ref[:, 0:1], 0.0)
    second = jnp.where(place == row + 1, scores_ref[:, 1:2], 0.0)
    out_ref[...] = jnp.sum(first + second, axis=0, keepdims=True)


def make_per_device(docs_axis, split_axis):
    devices = docs_axis * split_axis
    clusters = devices // 2
    slots = clusters * SLOTS

    groups = [
        [d * split_axis + s for d in range(core, docs_axis, 2) for s in range(split_axis)]
        for core in range(2)
    ]
    partner = [(d, d ^ 1) for d in range(docs_axis)]
    both = ("docs", "split")

    def per_device(embeddings, cluster_id, rank):
        docs, width = embeddings.shape
        wide = width + LANES
        send, place = pl.pallas_call(
            pack_kernel,
            out_shape=(
                jax.ShapeDtypeStruct((slots, wide), jnp.bfloat16),
                jax.ShapeDtypeStruct((1, docs), jnp.int32),
            ),
            in_specs=[pl.BlockSpec(memory_space=pltpu.HBM)] * 3,
            scratch_shapes=[
                pltpu.VMEM((docs, width), jnp.bfloat16),
                pltpu.VMEM((1, docs), jnp.int32),
                pltpu.VMEM((1, docs), jnp.int32),
                pltpu.SemaphoreType.DMA((3,)),
            ],
            name="pack", compiler_params=PARAMS,
        )(embeddings, cluster_id.reshape(1, docs), rank.reshape(1, docs))
        got = lax.all_to_all(
            send.reshape(clusters, SLOTS, wide), both, 0, 0, axis_index_groups=groups, tiled=True
        )
        queries = got.reshape(slots, wide)
        keys = lax.ppermute(queries, "docs", partner)
        best = pl.pallas_call(
            make_own(width), out_shape=jax.ShapeDtypeStruct((1, slots), jnp.float32), name="own", compiler_params=PARAMS
        )(queries)
        scores = pl.pallas_call(
            make_peer(width),
            out_shape=jax.ShapeDtypeStruct((clusters, LANES), jnp.float32),
            name="peer", compiler_params=PARAMS,
        )(queries, keys, best)
        back = lax.all_to_all(
            scores.reshape(clusters, 1, LANES), both, 0, 0, axis_index_groups=groups, tiled=True
        ).reshape(clusters, LANES)
        out = pl.pallas_call(
            unpack_kernel, out_shape=jax.ShapeDtypeStruct((1, docs), jnp.float32), name="unpack", compiler_params=PARAMS
        )(back, place)
        return out.reshape(docs)

    return per_device


def solution(mesh):
    placed = (P(("docs", "split"), None), P(("docs", "split")), P(("docs", "split")))
    per_device = make_per_device(mesh.shape["docs"], mesh.shape["split"])
    return jax.shard_map(
        per_device, mesh=mesh, in_specs=placed, out_specs=P(("docs", "split")), check_vma=False
    )
```

```python
import jax
import jax.numpy as jnp
from jax import lax
from jax.experimental import pallas as pl
from jax.experimental.pallas import tpu as pltpu
from jax.sharding import PartitionSpec as P

EPSILON = 1e-06
CL_DEV = 2
SLOTS = 2
LANES = 128
RANKS = 65536.0
SECOND = 2 * RANKS
SMALL = pltpu.CompilerParams(vmem_limit_bytes=16 << 20)
CONTRACT = (((1,), (1,)), ((), ()))


def pack_kernel(rows_ref, cluster_ref, rank_ref, send_ref, place_ref):
    docs, width = rows_ref.shape
    owners = send_ref.shape[0]
    row = lax.broadcasted_iota(jnp.int32, (docs, docs), 0)
    col = lax.broadcasted_iota(jnp.int32, (docs, docs), 1)
    cluster = jnp.broadcast_to(cluster_ref[...], (docs, docs))
    cluster_col = jnp.sum(jnp.where(row == col, cluster, 0), axis=1, keepdims=True)
    rank = jnp.broadcast_to(rank_ref[...], (docs, docs))
    rank_col = jnp.sum(jnp.where(row == col, rank, 0), axis=1, keepdims=True)
    owner = cluster_ref[...] // CL_DEV
    earlier = (cluster_col // CL_DEV == owner) & (row < col)
    slot = jnp.sum(earlier.astype(jnp.int32), axis=0, keepdims=True)
    place = owner * SLOTS + slot
    place_ref[...] = place
    target = lax.broadcasted_iota(jnp.int32, (owners * SLOTS, docs), 0)
    onehot = (target == place).astype(jnp.float32).astype(jnp.bfloat16)
    age = 65536 - rank_col
    high = age // 256
    low = age - high * 256
    lane = lax.broadcasted_iota(jnp.int32, (docs, LANES), 1)
    digits = jnp.where(lane == 0, high, jnp.where(lane == 1, low, jnp.where(lane == 2, cluster_col % CL_DEV, 0)))
    digits = digits.astype(jnp.float32).astype(jnp.bfloat16)
    codes = jnp.dot(onehot, digits, preferred_element_type=jnp.float32).astype(jnp.bfloat16)
    values = rows_ref[...].astype(jnp.float32)
    total = jnp.sum(values * values, axis=1, keepdims=True)
    unit = (values / jnp.sqrt(total + EPSILON)).astype(jnp.bfloat16)
    rows = jnp.dot(onehot, unit, preferred_element_type=jnp.float32).astype(jnp.bfloat16)
    send_ref[:, :, :width] = rows.reshape(owners, SLOTS, width)
    send_ref[:, :, width:] = codes.reshape(owners, SLOTS, LANES)


def code_weights(shape, axis):
    place = lax.broadcasted_iota(jnp.int32, shape, axis)
    weight = jnp.where(place == 0, 256.0, jnp.where(place == 1, 1.0, jnp.where(place == 2, SECOND, 0.0)))
    return weight.astype(jnp.bfloat16)


def query_codes(queries_ref, width):
    code = lax.dot_general(
        code_weights((8, LANES), 1), queries_ref[:, width:], CONTRACT, preferred_element_type=jnp.float32
    )[:1, :]
    return code, jnp.where(code > RANKS, SECOND + RANKS, RANKS)


def best_of(keys_ref, queries_ref, code, last, width):
    key_code = jnp.dot(keys_ref[:, width:], code_weights((LANES, LANES), 0), preferred_element_type=jnp.float32)
    key_code = key_code[:, :1]
    scores = lax.dot_general(
        keys_ref[:, :width], queries_ref[:, :width], CONTRACT, preferred_element_type=jnp.float32
    )
    allowed = (key_code > code) & (key_code <= last)
    return jnp.max(jnp.where(allowed, scores, -1.0), axis=0, keepdims=True)


def across_kernel(before_ref, after_ref, best_ref):
    width = before_ref.shape[1] - LANES
    code, last = query_codes(before_ref, width)
    best = best_of(after_ref, before_ref, code, last, width)
    best_ref[...] = jnp.broadcast_to(best, best_ref.shape)


def own_kernel(queries_ref, before_ref, after_ref, best_ref):
    width = queries_ref.shape[1] - LANES
    code, last = query_codes(queries_ref, width)
    best = best_of(queries_ref, queries_ref, code, last, width)
    best = jnp.maximum(best, best_of(before_ref, queries_ref, code, last, width))
    best = jnp.maximum(best, best_of(after_ref, queries_ref, code, last, width))
    best_ref[...] = jnp.broadcast_to(best, best_ref.shape)


def spread_kernel(own_ref, across_ref, out_ref):
    best = jnp.maximum(own_ref[:1, :], across_ref[:1, :])
    messages = out_ref.shape[0]
    count = best.shape[1]
    best = jnp.broadcast_to(best, (messages, count))
    row = lax.broadcasted_iota(jnp.int32, (messages, count), 0) * SLOTS
    col = lax.broadcasted_iota(jnp.int32, (messages, count), 1)
    first = jnp.sum(jnp.where(col == row, best, 0.0), axis=1, keepdims=True)
    second = jnp.sum(jnp.where(col == row + 1, best, 0.0), axis=1, keepdims=True)
    lane = lax.broadcasted_iota(jnp.int32, out_ref.shape, 1)
    out_ref[...] = jnp.where(lane == 0, first, second)


def unpack_kernel(scores_ref, place_ref, out_ref):
    owners = scores_ref.shape[0]
    docs = place_ref.shape[1]
    row = lax.broadcasted_iota(jnp.int32, (owners, docs), 0) * SLOTS
    first = jnp.where(place_ref[...] == row, scores_ref[:, 0:1], 0.0)
    second = jnp.where(place_ref[...] == row + 1, scores_ref[:, 1:2], 0.0)
    out_ref[...] = jnp.sum(first + second, axis=0, keepdims=True)


def make_per_device(owners, peers):
    slots = owners * SLOTS
    ahead = [(i, (i + 1) % peers) for i in range(peers)]
    behind = [(i, (i - 1) % peers) for i in range(peers)]
    row = jax.ShapeDtypeStruct((8, slots), jnp.float32)

    def per_device(embeddings, cluster_id, rank):
        docs, width = embeddings.shape
        wide = width + LANES
        send, place = pl.pallas_call(
            pack_kernel,
            out_shape=(
                jax.ShapeDtypeStruct((owners, SLOTS, wide), jnp.bfloat16),
                jax.ShapeDtypeStruct((1, docs), jnp.int32),
            ),
            name="pack",
        )(embeddings, cluster_id.reshape(1, docs), rank.reshape(1, docs))
        queries = lax.all_to_all(send, "docs", 0, 0, tiled=True).reshape(slots, wide)
        before = lax.ppermute(queries, "split", ahead)
        after = lax.ppermute(queries, "split", behind)
        across = pl.pallas_call(across_kernel, out_shape=row, compiler_params=SMALL, name="across")(before, after)
        across = lax.ppermute(across, "split", behind)
        own = pl.pallas_call(own_kernel, out_shape=row, compiler_params=SMALL, name="own")(queries, before, after)
        scores = pl.pallas_call(
            spread_kernel,
            out_shape=jax.ShapeDtypeStruct((owners, LANES), jnp.float32),
            compiler_params=SMALL,
            name="spread",
        )(own, across)
        back = lax.all_to_all(scores.reshape(owners, 1, LANES), "docs", 0, 0, tiled=True)
        out = pl.pallas_call(
            unpack_kernel,
            out_shape=jax.ShapeDtypeStruct((1, docs), jnp.float32),
            compiler_params=SMALL,
            name="unpack",
        )(back.reshape(owners, LANES), place)
        return out.reshape(docs)

    return per_device


def solution(mesh):
    placed = (P(("docs", "split"), None), P(("docs", "split")), P(("docs", "split")))
    assert mesh.shape["split"] == 4
    per_device = make_per_device(mesh.shape["docs"], mesh.shape["split"])
    return jax.shard_map(
        per_device, mesh=mesh, in_specs=placed, out_specs=P(("docs", "split")), check_vma=False
    )
```

```python
import jax
import jax.numpy as jnp
from jax import lax
from jax.experimental import pallas as pl
from jax.experimental.pallas import tpu as pltpu
from jax.sharding import PartitionSpec as P

EPSILON = 1e-06
SLOTS = 2
LANES = 128
PARAMS = pltpu.CompilerParams(vmem_limit_bytes=16 << 20)


def pack_kernel(rows_hbm, cluster_hbm, rank_hbm, send_ref, place_ref, rows_ref, cluster_ref, rank_ref, sems):
    load_cluster = pltpu.make_async_copy(cluster_hbm, cluster_ref, sems.at[0])
    load_rank = pltpu.make_async_copy(rank_hbm, rank_ref, sems.at[1])
    load_rows = pltpu.make_async_copy(rows_hbm, rows_ref, sems.at[2])
    load_cluster.start()
    load_rank.start()
    load_rows.start()
    docs, width = rows_ref.shape
    clusters = send_ref.shape[0]
    slots = clusters * SLOTS
    row = lax.broadcasted_iota(jnp.int32, (docs, docs), 0)
    col = lax.broadcasted_iota(jnp.int32, (docs, docs), 1)
    lane = lax.broadcasted_iota(jnp.int32, (docs, LANES), 1)
    target = lax.broadcasted_iota(jnp.int32, (slots, docs), 0)
    load_cluster.wait()
    cluster = jnp.broadcast_to(cluster_ref[...], (docs, docs))
    cluster_col = jnp.sum(jnp.where(row == col, cluster, 0), axis=1, keepdims=True)
    earlier = (cluster_col == cluster) & (row < col)
    slot = jnp.sum(earlier.astype(jnp.int32), axis=0, keepdims=True)
    place = cluster_ref[...] * SLOTS + slot
    place_ref[...] = place
    onehot = (target == jnp.broadcast_to(place, (slots, docs))).astype(jnp.float32).astype(jnp.bfloat16)
    load_rank.wait()
    rank = jnp.broadcast_to(rank_ref[...], (docs, docs))
    age = 65536 - jnp.sum(jnp.where(row == col, rank, 0), axis=1, keepdims=True)
    high = age // 256
    low = age - high * 256
    digits = jnp.where(lane == 0, high, jnp.where(lane == 1, low, 0))
    digits = digits.astype(jnp.float32).astype(jnp.bfloat16)
    digits = jnp.dot(onehot, digits, preferred_element_type=jnp.float32).astype(jnp.bfloat16)
    send_ref[:, :, width:] = digits.reshape(clusters, SLOTS, LANES)
    load_rows.wait()
    values = rows_ref[...].astype(jnp.float32)
    total = jnp.sum(values * values, axis=1, keepdims=True)
    unit = (values / jnp.sqrt(total + EPSILON)).astype(jnp.bfloat16)
    rows = jnp.dot(onehot, unit, preferred_element_type=jnp.float32).astype(jnp.bfloat16)
    send_ref[:, :, :width] = rows.reshape(clusters, SLOTS, width)


def age_weights(shape, axis):
    place = lax.broadcasted_iota(jnp.int32, shape, axis)
    return jnp.where(place == 0, 256.0, jnp.where(place == 1, 1.0, 0.0)).astype(jnp.bfloat16)


def best_of(keys_ref, queries_ref, width):
    contract = (((1,), (1,)), ((), ()))
    key_age = jnp.dot(keys_ref[:, width:], age_weights((LANES, LANES), 0), preferred_element_type=jnp.float32)
    query_age = lax.dot_general(
        age_weights((8, LANES), 1), queries_ref[:, width:], contract, preferred_element_type=jnp.float32
    )
    scores = lax.dot_general(
        keys_ref[:, :width], queries_ref[:, :width], contract, preferred_element_type=jnp.float32
    )
    allowed = key_age[:, :1] > query_age[:1, :]
    return jnp.max(jnp.where(allowed, scores, -1.0), axis=0, keepdims=True)


def make_own(width):
    def kernel(queries_ref, best_ref):
        best_ref[...] = best_of(queries_ref, queries_ref, width)

    return kernel


def make_peer(width):
    def kernel(queries_ref, keys_ref, best_ref, out_ref):
        best = jnp.maximum(best_ref[...], best_of(keys_ref, queries_ref, width))
        messages = out_ref.shape[0]
        count = best.shape[1]
        best = jnp.broadcast_to(best, (messages, count))
        row = lax.broadcasted_iota(jnp.int32, (messages, count), 0) * SLOTS
        col = lax.broadcasted_iota(jnp.int32, (messages, count), 1)
        first = jnp.sum(jnp.where(col == row, best, 0.0), axis=1, keepdims=True)
        second = jnp.sum(jnp.where(col == row + 1, best, 0.0), axis=1, keepdims=True)
        lane = lax.broadcasted_iota(jnp.int32, out_ref.shape, 1)
        out_ref[...] = jnp.where(lane == 0, first, second)

    return kernel


def unpack_kernel(scores_ref, place_ref, out_ref):
    clusters = scores_ref.shape[0]
    docs = place_ref.shape[1]
    place = jnp.broadcast_to(place_ref[...], (clusters, docs))
    row = lax.broadcasted_iota(jnp.int32, (clusters, docs), 0) * SLOTS
    first = jnp.where(place == row, scores_ref[:, 0:1], 0.0)
    second = jnp.where(place == row + 1, scores_ref[:, 1:2], 0.0)
    out_ref[...] = jnp.sum(first + second, axis=0, keepdims=True)


def make_per_device(docs_axis, split_axis):
    devices = docs_axis * split_axis
    clusters = devices // 2
    slots = clusters * SLOTS

    groups = [
        [d * split_axis + s for d in range(core, docs_axis, 2) for s in range(split_axis)]
        for core in range(2)
    ]
    partner = [(d, d ^ 1) for d in range(docs_axis)]
    both = ("docs", "split")

    def per_device(embeddings, cluster_id, rank):
        docs, width = embeddings.shape
        wide = width + LANES
        send, place = pl.pallas_call(
            pack_kernel,
            out_shape=(
                jax.ShapeDtypeStruct((clusters, SLOTS, wide), jnp.bfloat16),
                jax.ShapeDtypeStruct((1, docs), jnp.int32),
            ),
            in_specs=[pl.BlockSpec(memory_space=pltpu.HBM)] * 3,
            scratch_shapes=[
                pltpu.VMEM((docs, width), jnp.bfloat16),
                pltpu.VMEM((1, docs), jnp.int32),
                pltpu.VMEM((1, docs), jnp.int32),
                pltpu.SemaphoreType.DMA((3,)),
            ],
            name="pack", compiler_params=PARAMS,
        )(
            pltpu.with_memory_space_constraint(embeddings, pltpu.HBM),
            pltpu.with_memory_space_constraint(cluster_id.reshape(1, docs), pltpu.HBM),
            pltpu.with_memory_space_constraint(rank.reshape(1, docs), pltpu.HBM),
        )
        got = lax.all_to_all(
            send, both, 0, 0, axis_index_groups=groups, tiled=True
        )
        queries = got.reshape(slots, wide)
        keys = lax.ppermute(queries, "docs", partner)
        best = pl.pallas_call(
            make_own(width), out_shape=jax.ShapeDtypeStruct((1, slots), jnp.float32), name="own", compiler_params=PARAMS
        )(queries)
        scores = pl.pallas_call(
            make_peer(width),
            out_shape=jax.ShapeDtypeStruct((clusters, LANES), jnp.float32),
            name="peer", compiler_params=PARAMS,
        )(queries, keys, best)
        back = lax.all_to_all(
            scores.reshape(clusters, 1, LANES), both, 0, 0, axis_index_groups=groups, tiled=True
        ).reshape(clusters, LANES)
        out = pl.pallas_call(
            unpack_kernel, out_shape=jax.ShapeDtypeStruct((1, docs), jnp.float32), name="unpack", compiler_params=PARAMS
        )(back, place)
        return out.reshape(docs)

    return per_device


def solution(mesh):
    placed = (P(("docs", "split"), None), P(("docs", "split")), P(("docs", "split")))
    per_device = make_per_device(mesh.shape["docs"], mesh.shape["split"])
    return jax.shard_map(
        per_device, mesh=mesh, in_specs=placed, out_specs=P(("docs", "split")), check_vma=False
    )
```

```python
import jax
import jax.numpy as jnp
from jax import lax
from jax.experimental import pallas as pl
from jax.experimental.pallas import tpu as pltpu
from jax.sharding import PartitionSpec as P

EPSILON = 1e-06
CL_DEV = 2
SLOTS = 2
LANES = 128
RANKS = 65536.0
SECOND = 2 * RANKS
SMALL = pltpu.CompilerParams(vmem_limit_bytes=16 << 20)
CONTRACT = (((1,), (1,)), ((), ()))


def pack_kernel(rows_hbm, cluster_hbm, rank_hbm, send_ref, place_ref, rows_ref, cluster_ref, rank_ref, sems):
    load_cluster = pltpu.make_async_copy(cluster_hbm, cluster_ref, sems.at[0])
    load_rank = pltpu.make_async_copy(rank_hbm, rank_ref, sems.at[1])
    load_rows = pltpu.make_async_copy(rows_hbm, rows_ref, sems.at[2])
    load_cluster.start()
    load_rank.start()
    load_rows.start()
    docs, width = rows_ref.shape
    owners = send_ref.shape[0]
    row = lax.broadcasted_iota(jnp.int32, (docs, docs), 0)
    col = lax.broadcasted_iota(jnp.int32, (docs, docs), 1)
    lane = lax.broadcasted_iota(jnp.int32, (docs, LANES), 1)
    target = lax.broadcasted_iota(jnp.int32, (owners * SLOTS, docs), 0)
    load_cluster.wait()
    cluster = jnp.broadcast_to(cluster_ref[...], (docs, docs))
    cluster_col = jnp.sum(jnp.where(row == col, cluster, 0), axis=1, keepdims=True)
    owner = cluster_ref[...] // CL_DEV
    earlier = (cluster_col // CL_DEV == owner) & (row < col)
    slot = jnp.sum(earlier.astype(jnp.int32), axis=0, keepdims=True)
    place = owner * SLOTS + slot
    place_ref[...] = place
    onehot = (target == place).astype(jnp.float32).astype(jnp.bfloat16)
    load_rank.wait()
    rank = jnp.broadcast_to(rank_ref[...], (docs, docs))
    age = 65536 - jnp.sum(jnp.where(row == col, rank, 0), axis=1, keepdims=True)
    high = age // 256
    low = age - high * 256
    digits = jnp.where(lane == 0, high, jnp.where(lane == 1, low, jnp.where(lane == 2, cluster_col % CL_DEV, 0)))
    digits = digits.astype(jnp.float32).astype(jnp.bfloat16)
    codes = jnp.dot(onehot, digits, preferred_element_type=jnp.float32).astype(jnp.bfloat16)
    send_ref[:, :, width:] = codes.reshape(owners, SLOTS, LANES)
    load_rows.wait()
    values = rows_ref[...].astype(jnp.float32)
    total = jnp.sum(values * values, axis=1, keepdims=True)
    unit = (values / jnp.sqrt(total + EPSILON)).astype(jnp.bfloat16)
    rows = jnp.dot(onehot, unit, preferred_element_type=jnp.float32).astype(jnp.bfloat16)
    send_ref[:, :, :width] = rows.reshape(owners, SLOTS, width)


def code_weights(shape, axis):
    place = lax.broadcasted_iota(jnp.int32, shape, axis)
    weight = jnp.where(place == 0, 256.0, jnp.where(place == 1, 1.0, jnp.where(place == 2, SECOND, 0.0)))
    return weight.astype(jnp.bfloat16)


def query_codes(queries_ref, width):
    code = lax.dot_general(
        code_weights((8, LANES), 1), queries_ref[:, width:], CONTRACT, preferred_element_type=jnp.float32
    )[:1, :]
    return code, jnp.where(code > RANKS, SECOND + RANKS, RANKS)


def best_of(keys_ref, queries_ref, code, last, width):
    key_code = jnp.dot(keys_ref[:, width:], code_weights((LANES, LANES), 0), preferred_element_type=jnp.float32)
    key_code = key_code[:, :1]
    scores = lax.dot_general(
        keys_ref[:, :width], queries_ref[:, :width], CONTRACT, preferred_element_type=jnp.float32
    )
    allowed = (key_code > code) & (key_code <= last)
    return jnp.max(jnp.where(allowed, scores, -1.0), axis=0, keepdims=True)


def across_kernel(before_ref, after_ref, best_ref):
    width = before_ref.shape[1] - LANES
    code, last = query_codes(before_ref, width)
    best = best_of(after_ref, before_ref, code, last, width)
    best_ref[...] = jnp.broadcast_to(best, best_ref.shape)


def own_kernel(queries_ref, before_ref, after_ref, best_ref):
    width = queries_ref.shape[1] - LANES
    code, last = query_codes(queries_ref, width)
    best = best_of(queries_ref, queries_ref, code, last, width)
    best = jnp.maximum(best, best_of(before_ref, queries_ref, code, last, width))
    best = jnp.maximum(best, best_of(after_ref, queries_ref, code, last, width))
    best_ref[...] = jnp.broadcast_to(best, best_ref.shape)


def spread_kernel(own_ref, across_ref, out_ref):
    best = jnp.maximum(own_ref[:1, :], across_ref[:1, :])
    messages = out_ref.shape[0]
    count = best.shape[1]
    best = jnp.broadcast_to(best, (messages, count))
    row = lax.broadcasted_iota(jnp.int32, (messages, count), 0) * SLOTS
    col = lax.broadcasted_iota(jnp.int32, (messages, count), 1)
    first = jnp.sum(jnp.where(col == row, best, 0.0), axis=1, keepdims=True)
    second = jnp.sum(jnp.where(col == row + 1, best, 0.0), axis=1, keepdims=True)
    lane = lax.broadcasted_iota(jnp.int32, out_ref.shape, 1)
    out_ref[...] = jnp.where(lane == 0, first, second)


def unpack_kernel(scores_ref, place_ref, out_ref):
    owners = scores_ref.shape[0]
    docs = place_ref.shape[1]
    row = lax.broadcasted_iota(jnp.int32, (owners, docs), 0) * SLOTS
    first = jnp.where(place_ref[...] == row, scores_ref[:, 0:1], 0.0)
    second = jnp.where(place_ref[...] == row + 1, scores_ref[:, 1:2], 0.0)
    out_ref[...] = jnp.sum(first + second, axis=0, keepdims=True)


RING = {(0, 0): 0, (0, 1): 1, (1, 1): 2, (1, 0): 3}


def layout(side_y, side_z, side_x):
    table = {}
    for y in range(side_y):
        for z in range(side_z):
            for core in range(2):
                sy, sz = (y + core) % side_y, (z + core) % side_z
                square = (sy // 2) * (side_z // 2) + sz // 2
                for x in range(side_x):
                    owner = (x * (side_y // 2) * (side_z // 2) + square) * 2 + core
                    device = ((y * side_z + z) * 2 + core) * side_x + x
                    table[RING[sy % 2, sz % 2], owner] = device
    owners = max(owner for _, owner in table) + 1
    groups = [[table[member, owner] for owner in range(owners)] for member in range(4)]
    ahead = [(table[m, o], table[(m + 1) % 4, o]) for m in range(4) for o in range(owners)]
    behind = [(b, a) for a, b in ahead]
    return owners, groups, ahead, behind


def make_per_device(docs_axis, split_axis):
    side = round((docs_axis // 2) ** 0.5)
    owners, groups, ahead, behind = layout(side, side, split_axis)
    slots = owners * SLOTS
    both = ("docs", "split")
    row = jax.ShapeDtypeStruct((8, slots), jnp.float32)

    def per_device(embeddings, cluster_id, rank):
        docs, width = embeddings.shape
        wide = width + LANES
        send, place = pl.pallas_call(
            pack_kernel,
            out_shape=(
                jax.ShapeDtypeStruct((owners, SLOTS, wide), jnp.bfloat16),
                jax.ShapeDtypeStruct((1, docs), jnp.int32),
            ),
            in_specs=[pl.BlockSpec(memory_space=pltpu.HBM)] * 3,
            scratch_shapes=[
                pltpu.VMEM((docs, width), jnp.bfloat16),
                pltpu.VMEM((1, docs), jnp.int32),
                pltpu.VMEM((1, docs), jnp.int32),
                pltpu.SemaphoreType.DMA((3,)),
            ],
            compiler_params=SMALL,
            name="pack",
        )(
            pltpu.with_memory_space_constraint(embeddings, pltpu.HBM),
            pltpu.with_memory_space_constraint(cluster_id.reshape(1, docs), pltpu.HBM),
            pltpu.with_memory_space_constraint(rank.reshape(1, docs), pltpu.HBM),
        )
        got = lax.all_to_all(send, both, 0, 0, axis_index_groups=groups, tiled=True)
        queries = got.reshape(slots, wide)
        before = lax.ppermute(queries, both, ahead)
        after = lax.ppermute(queries, both, behind)
        across = pl.pallas_call(across_kernel, out_shape=row, compiler_params=SMALL, name="across")(before, after)
        across = lax.ppermute(across, both, behind)
        own = pl.pallas_call(own_kernel, out_shape=row, compiler_params=SMALL, name="own")(queries, before, after)
        scores = pl.pallas_call(
            spread_kernel,
            out_shape=jax.ShapeDtypeStruct((owners, LANES), jnp.float32),
            compiler_params=SMALL,
            name="spread",
        )(own, across)
        back = lax.all_to_all(
            scores.reshape(owners, 1, LANES), both, 0, 0, axis_index_groups=groups, tiled=True
        )
        out = pl.pallas_call(
            unpack_kernel,
            out_shape=jax.ShapeDtypeStruct((1, docs), jnp.float32),
            compiler_params=SMALL,
            name="unpack",
        )(back.reshape(owners, LANES), place)
        return out.reshape(docs)

    return per_device


def solution(mesh):
    placed = (P(("docs", "split"), None), P(("docs", "split")), P(("docs", "split")))
    per_device = make_per_device(mesh.shape["docs"], mesh.shape["split"])
    return jax.shard_map(
        per_device, mesh=mesh, in_specs=placed, out_specs=P(("docs", "split")), check_vma=False
    )
```

```python
import jax
import jax.numpy as jnp
from jax import lax
from jax.experimental import pallas as pl
from jax.experimental.pallas import tpu as pltpu
from jax.sharding import PartitionSpec as P

EPSILON = 1e-06
CL_DEV = 2
SLOTS = 2
LANES = 128
RANKS = 65536.0
SECOND = 2 * RANKS
SMALL = pltpu.CompilerParams(vmem_limit_bytes=16 << 20)
CONTRACT = (((1,), (1,)), ((), ()))


def pack_kernel(rows_hbm, cluster_hbm, rank_hbm, send_ref, place_ref, rows_ref, cluster_ref, rank_ref, sems):
    load_cluster = pltpu.make_async_copy(cluster_hbm, cluster_ref, sems.at[0])
    load_rank = pltpu.make_async_copy(rank_hbm, rank_ref, sems.at[1])
    load_rows = pltpu.make_async_copy(rows_hbm, rows_ref, sems.at[2])
    load_cluster.start()
    load_rank.start()
    load_rows.start()
    docs, width = rows_ref.shape
    owners = send_ref.shape[0]
    row = lax.broadcasted_iota(jnp.int32, (docs, docs), 0)
    col = lax.broadcasted_iota(jnp.int32, (docs, docs), 1)
    lane = lax.broadcasted_iota(jnp.int32, (docs, LANES), 1)
    target = lax.broadcasted_iota(jnp.int32, (owners * SLOTS, docs), 0)
    load_cluster.wait()
    cluster = jnp.broadcast_to(cluster_ref[...], (docs, docs))
    cluster_col = jnp.sum(jnp.where(row == col, cluster, 0), axis=1, keepdims=True)
    owner = cluster_ref[...] // CL_DEV
    earlier = (cluster_col // CL_DEV == owner) & (row < col)
    slot = jnp.sum(earlier.astype(jnp.int32), axis=0, keepdims=True)
    place = owner * SLOTS + slot
    place_ref[...] = place
    onehot = (target == place).astype(jnp.float32).astype(jnp.bfloat16)
    load_rank.wait()
    rank = jnp.broadcast_to(rank_ref[...], (docs, docs))
    age = 65536 - jnp.sum(jnp.where(row == col, rank, 0), axis=1, keepdims=True)
    high = age // 256
    low = age - high * 256
    digits = jnp.where(lane == 0, high, jnp.where(lane == 1, low, jnp.where(lane == 2, cluster_col % CL_DEV, 0)))
    digits = digits.astype(jnp.float32).astype(jnp.bfloat16)
    codes = jnp.dot(onehot, digits, preferred_element_type=jnp.float32).astype(jnp.bfloat16)
    send_ref[:, :, width:] = codes.reshape(owners, SLOTS, LANES)
    load_rows.wait()
    values = rows_ref[...].astype(jnp.float32)
    total = jnp.sum(values * values, axis=1, keepdims=True)
    unit = (values / jnp.sqrt(total + EPSILON)).astype(jnp.bfloat16)
    rows = jnp.dot(onehot, unit, preferred_element_type=jnp.float32).astype(jnp.bfloat16)
    send_ref[:, :, :width] = rows.reshape(owners, SLOTS, width)


def code_weights(shape, axis):
    place = lax.broadcasted_iota(jnp.int32, shape, axis)
    weight = jnp.where(place == 0, 256.0, jnp.where(place == 1, 1.0, jnp.where(place == 2, SECOND, 0.0)))
    return weight.astype(jnp.bfloat16)


def query_codes(queries_ref, width):
    code = lax.dot_general(
        code_weights((8, LANES), 1), queries_ref[:, width:], CONTRACT, preferred_element_type=jnp.float32
    )[:1, :]
    return code, jnp.where(code > RANKS, SECOND + RANKS, RANKS)


def best_of(keys_ref, queries_ref, code, last, width):
    key_code = jnp.dot(keys_ref[:, width:], code_weights((LANES, LANES), 0), preferred_element_type=jnp.float32)
    key_code = key_code[:, :1]
    scores = lax.dot_general(
        keys_ref[:, :width], queries_ref[:, :width], CONTRACT, preferred_element_type=jnp.float32
    )
    allowed = (key_code > code) & (key_code <= last)
    return jnp.max(jnp.where(allowed, scores, -1.0), axis=0, keepdims=True)


def near_kernel(queries_ref, before_ref, after_ref, best_ref):
    width = queries_ref.shape[1] - LANES
    code, last = query_codes(queries_ref, width)
    best = best_of(queries_ref, queries_ref, code, last, width)
    best = jnp.maximum(best, best_of(before_ref, queries_ref, code, last, width))
    best_ref[...] = jnp.maximum(best, best_of(after_ref, queries_ref, code, last, width))


def far_kernel(queries_ref, across_ref, best_ref, out_ref):
    width = queries_ref.shape[1] - LANES
    code, last = query_codes(queries_ref, width)
    best = jnp.maximum(best_ref[...], best_of(across_ref, queries_ref, code, last, width))
    messages = out_ref.shape[0]
    count = best.shape[1]
    best = jnp.broadcast_to(best, (messages, count))
    row = lax.broadcasted_iota(jnp.int32, (messages, count), 0) * SLOTS
    col = lax.broadcasted_iota(jnp.int32, (messages, count), 1)
    first = jnp.sum(jnp.where(col == row, best, 0.0), axis=1, keepdims=True)
    second = jnp.sum(jnp.where(col == row + 1, best, 0.0), axis=1, keepdims=True)
    lane = lax.broadcasted_iota(jnp.int32, out_ref.shape, 1)
    out_ref[...] = jnp.where(lane == 0, first, second)


def unpack_kernel(scores_ref, place_ref, out_ref):
    owners = scores_ref.shape[0]
    docs = place_ref.shape[1]
    row = lax.broadcasted_iota(jnp.int32, (owners, docs), 0) * SLOTS
    first = jnp.where(place_ref[...] == row, scores_ref[:, 0:1], 0.0)
    second = jnp.where(place_ref[...] == row + 1, scores_ref[:, 1:2], 0.0)
    out_ref[...] = jnp.sum(first + second, axis=0, keepdims=True)


RING = {(0, 0): 0, (0, 1): 1, (1, 1): 2, (1, 0): 3}


def layout(side_y, side_z, side_x):
    table = {}
    for y in range(side_y):
        for z in range(side_z):
            for core in range(2):
                sy, sz = (y + core) % side_y, (z + core) % side_z
                square = (sy // 2) * (side_z // 2) + sz // 2
                for x in range(side_x):
                    owner = (x * (side_y // 2) * (side_z // 2) + square) * 2 + core
                    device = ((y * side_z + z) * 2 + core) * side_x + x
                    table[RING[sy % 2, sz % 2], owner] = device
    owners = max(owner for _, owner in table) + 1
    groups = [[table[member, owner] for owner in range(owners)] for member in range(4)]
    ahead = [(table[m, o], table[(m + 1) % 4, o]) for m in range(4) for o in range(owners)]
    behind = [(b, a) for a, b in ahead]
    opposite = [(table[m, o], table[(m + 2) % 4, o]) for m in range(4) for o in range(owners)]
    return owners, groups, ahead, behind, opposite


def make_per_device(docs_axis, split_axis):
    side = round((docs_axis // 2) ** 0.5)
    owners, groups, ahead, behind, opposite = layout(side, side, split_axis)
    slots = owners * SLOTS
    both = ("docs", "split")

    def per_device(embeddings, cluster_id, rank):
        docs, width = embeddings.shape
        wide = width + LANES
        send, place = pl.pallas_call(
            pack_kernel,
            out_shape=(
                jax.ShapeDtypeStruct((owners, SLOTS, wide), jnp.bfloat16),
                jax.ShapeDtypeStruct((1, docs), jnp.int32),
            ),
            in_specs=[pl.BlockSpec(memory_space=pltpu.HBM)] * 3,
            scratch_shapes=[
                pltpu.VMEM((docs, width), jnp.bfloat16),
                pltpu.VMEM((1, docs), jnp.int32),
                pltpu.VMEM((1, docs), jnp.int32),
                pltpu.SemaphoreType.DMA((3,)),
            ],
            compiler_params=SMALL,
            name="pack",
        )(
            pltpu.with_memory_space_constraint(embeddings, pltpu.HBM),
            pltpu.with_memory_space_constraint(cluster_id.reshape(1, docs), pltpu.HBM),
            pltpu.with_memory_space_constraint(rank.reshape(1, docs), pltpu.HBM),
        )
        got = lax.all_to_all(send, both, 0, 0, axis_index_groups=groups, tiled=True)
        queries = got.reshape(slots, wide)
        before = lax.ppermute(queries, both, ahead)
        after = lax.ppermute(queries, both, behind)
        across = lax.ppermute(queries, both, opposite)
        best = pl.pallas_call(
            near_kernel,
            out_shape=jax.ShapeDtypeStruct((1, slots), jnp.float32),
            compiler_params=SMALL,
            name="near",
        )(queries, before, after)
        scores = pl.pallas_call(
            far_kernel,
            out_shape=jax.ShapeDtypeStruct((owners, LANES), jnp.float32),
            compiler_params=SMALL,
            name="far",
        )(queries, across, best)
        back = lax.all_to_all(
            scores.reshape(owners, 1, LANES), both, 0, 0, axis_index_groups=groups, tiled=True
        )
        out = pl.pallas_call(
            unpack_kernel,
            out_shape=jax.ShapeDtypeStruct((1, docs), jnp.float32),
            compiler_params=SMALL,
            name="unpack",
        )(back.reshape(owners, LANES), place)
        return out.reshape(docs)

    return per_device


def solution(mesh):
    placed = (P(("docs", "split"), None), P(("docs", "split")), P(("docs", "split")))
    per_device = make_per_device(mesh.shape["docs"], mesh.shape["split"])
    return jax.shard_map(
        per_device, mesh=mesh, in_specs=placed, out_specs=P(("docs", "split")), check_vma=False
    )
```

```python
import jax
import jax.numpy as jnp
from jax import lax
from jax.experimental import pallas as pl
from jax.experimental.pallas import tpu as pltpu
from jax.sharding import PartitionSpec as P

EPSILON = 1e-06
SLOTS = 2
LANES = 128
PARAMS = pltpu.CompilerParams(vmem_limit_bytes=16 << 20)


def pack_kernel(rows_hbm, cluster_hbm, rank_hbm, send_ref, place_ref, rows_ref, cluster_ref, rank_ref, sems):
    load_cluster = pltpu.make_async_copy(cluster_hbm, cluster_ref, sems.at[0])
    load_rank = pltpu.make_async_copy(rank_hbm, rank_ref, sems.at[1])
    load_rows = pltpu.make_async_copy(rows_hbm, rows_ref, sems.at[2])
    load_cluster.start()
    load_rank.start()
    load_rows.start()
    docs, width = rows_ref.shape
    clusters = send_ref.shape[0]
    slots = clusters * SLOTS
    row = lax.broadcasted_iota(jnp.int32, (docs, docs), 0)
    col = lax.broadcasted_iota(jnp.int32, (docs, docs), 1)
    lane = lax.broadcasted_iota(jnp.int32, (docs, LANES), 1)
    target = lax.broadcasted_iota(jnp.int32, (slots, docs), 0)
    load_cluster.wait()
    cluster = jnp.broadcast_to(cluster_ref[...], (docs, docs))
    cluster_col = jnp.sum(jnp.where(row == col, cluster, 0), axis=1, keepdims=True)
    earlier = (cluster_col == cluster) & (row < col)
    slot = jnp.sum(earlier.astype(jnp.int32), axis=0, keepdims=True)
    place = cluster_ref[...] * SLOTS + slot
    place_ref[...] = place
    onehot = (target == jnp.broadcast_to(place, (slots, docs))).astype(jnp.float32).astype(jnp.bfloat16)
    load_rank.wait()
    rank = jnp.broadcast_to(rank_ref[...], (docs, docs))
    age = 65536 - jnp.sum(jnp.where(row == col, rank, 0), axis=1, keepdims=True)
    high = age // 256
    low = age - high * 256
    digits = jnp.where(lane == 0, high, jnp.where(lane == 1, low, 0))
    digits = digits.astype(jnp.float32).astype(jnp.bfloat16)
    digits = jnp.dot(onehot, digits, preferred_element_type=jnp.float32).astype(jnp.bfloat16)
    send_ref[:, :, width:] = digits.reshape(clusters, SLOTS, LANES)
    load_rows.wait()
    values = rows_ref[...].astype(jnp.float32)
    total = jnp.sum(values * values, axis=1, keepdims=True)
    unit = (values / jnp.sqrt(total + EPSILON)).astype(jnp.bfloat16)
    rows = jnp.dot(onehot, unit, preferred_element_type=jnp.float32).astype(jnp.bfloat16)
    send_ref[:, :, :width] = rows.reshape(clusters, SLOTS, width)


def age_weights(shape, axis):
    place = lax.broadcasted_iota(jnp.int32, shape, axis)
    return jnp.where(place == 0, 256.0, jnp.where(place == 1, 1.0, 0.0)).astype(jnp.bfloat16)


def best_of(keys, queries_ref, width):
    contract = (((1,), (1,)), ((), ()))
    key_age = jnp.dot(keys[:, width:], age_weights((LANES, LANES), 0), preferred_element_type=jnp.float32)
    query_age = lax.dot_general(
        age_weights((8, LANES), 1), queries_ref[:, width:], contract, preferred_element_type=jnp.float32
    )
    scores = lax.dot_general(keys[:, :width], queries_ref[:, :width], contract, preferred_element_type=jnp.float32)
    allowed = key_age[:, :1] > query_age[:1, :]
    return jnp.max(jnp.where(allowed, scores, -1.0), axis=0, keepdims=True)


def make_own(width):
    def kernel(got_ref, queries_ref, best_ref):
        queries_ref[...] = got_ref[...].reshape(queries_ref.shape)
        best_ref[...] = best_of(queries_ref, queries_ref, width)

    return kernel


def make_peer(width):
    def kernel(queries_ref, keys_ref, best_ref, out_ref):
        best = jnp.maximum(best_ref[...], best_of(keys_ref[...].reshape(queries_ref.shape), queries_ref, width))
        messages = out_ref.shape[0]
        count = best.shape[1]
        best = jnp.broadcast_to(best, (messages, count))
        row = lax.broadcasted_iota(jnp.int32, (messages, count), 0) * SLOTS
        col = lax.broadcasted_iota(jnp.int32, (messages, count), 1)
        first = jnp.sum(jnp.where(col == row, best, 0.0), axis=1, keepdims=True)
        second = jnp.sum(jnp.where(col == row + 1, best, 0.0), axis=1, keepdims=True)
        lane = lax.broadcasted_iota(jnp.int32, out_ref.shape, 1)
        out_ref[...] = jnp.where(lane == 0, first, second)

    return kernel


def unpack_kernel(scores_ref, place_ref, out_ref):
    clusters = scores_ref.shape[0]
    docs = place_ref.shape[1]
    place = jnp.broadcast_to(place_ref[...], (clusters, docs))
    row = lax.broadcasted_iota(jnp.int32, (clusters, docs), 0) * SLOTS
    first = jnp.where(place == row, scores_ref[:, 0:1], 0.0)
    second = jnp.where(place == row + 1, scores_ref[:, 1:2], 0.0)
    out_ref[...] = jnp.sum(first + second, axis=0, keepdims=True)


def make_per_device(docs_axis, split_axis):
    devices = docs_axis * split_axis
    clusters = devices // 2
    slots = clusters * SLOTS

    groups = [
        [d * split_axis + s for d in range(core, docs_axis, 2) for s in range(split_axis)]
        for core in range(2)
    ]
    partner = [(d, d ^ 1) for d in range(docs_axis)]
    both = ("docs", "split")

    def per_device(embeddings, cluster_id, rank):
        docs, width = embeddings.shape
        wide = width + LANES
        send, place = pl.pallas_call(
            pack_kernel,
            out_shape=(
                jax.ShapeDtypeStruct((clusters, SLOTS, wide), jnp.bfloat16),
                jax.ShapeDtypeStruct((1, docs), jnp.int32),
            ),
            in_specs=[pl.BlockSpec(memory_space=pltpu.HBM)] * 3,
            scratch_shapes=[
                pltpu.VMEM((docs, width), jnp.bfloat16),
                pltpu.VMEM((1, docs), jnp.int32),
                pltpu.VMEM((1, docs), jnp.int32),
                pltpu.SemaphoreType.DMA((3,)),
            ],
            name="pack", compiler_params=PARAMS,
        )(
            pltpu.with_memory_space_constraint(embeddings, pltpu.HBM),
            pltpu.with_memory_space_constraint(cluster_id.reshape(1, docs), pltpu.HBM),
            pltpu.with_memory_space_constraint(rank.reshape(1, docs), pltpu.HBM),
        )
        got = lax.all_to_all(send, both, 0, 0, axis_index_groups=groups, tiled=True)
        keys = lax.ppermute(got, "docs", partner)
        queries, best = pl.pallas_call(
            make_own(width),
            out_shape=(
                jax.ShapeDtypeStruct((slots, wide), jnp.bfloat16),
                jax.ShapeDtypeStruct((1, slots), jnp.float32),
            ),
            name="own",
            compiler_params=PARAMS,
        )(got)
        scores = pl.pallas_call(
            make_peer(width),
            out_shape=jax.ShapeDtypeStruct((clusters, LANES), jnp.float32),
            name="peer", compiler_params=PARAMS,
        )(queries, keys, best)
        back = lax.all_to_all(
            scores.reshape(clusters, 1, LANES), both, 0, 0, axis_index_groups=groups, tiled=True
        ).reshape(clusters, LANES)
        out = pl.pallas_call(
            unpack_kernel, out_shape=jax.ShapeDtypeStruct((1, docs), jnp.float32), name="unpack", compiler_params=PARAMS
        )(back, place)
        return out.reshape(docs)

    return per_device


def solution(mesh):
    placed = (P(("docs", "split"), None), P(("docs", "split")), P(("docs", "split")))
    per_device = make_per_device(mesh.shape["docs"], mesh.shape["split"])
    return jax.shard_map(
        per_device, mesh=mesh, in_specs=placed, out_specs=P(("docs", "split")), check_vma=False
    )
```

```python
import jax
import jax.numpy as jnp
from jax import lax
from jax.experimental import pallas as pl
from jax.experimental.pallas import tpu as pltpu
from jax.sharding import PartitionSpec as P

EPSILON = 1e-06
SLOTS = 2
LANES = 128
PARAMS = pltpu.CompilerParams(vmem_limit_bytes=16 << 20)
PACKED = pltpu.CompilerParams(vmem_limit_bytes=16 << 20)


def pack_kernel(rows_hbm, cluster_hbm, rank_hbm, send_ref, place_ref, rows_ref, cluster_ref, rank_ref, sems):
    load_cluster = pltpu.make_async_copy(cluster_hbm, cluster_ref, sems.at[0])
    load_rank = pltpu.make_async_copy(rank_hbm, rank_ref, sems.at[1])
    load_rows = pltpu.make_async_copy(rows_hbm, rows_ref, sems.at[2])
    load_cluster.start()
    load_rank.start()
    load_rows.start()
    docs, width = rows_ref.shape
    clusters = send_ref.shape[0]
    slots = clusters * SLOTS
    row = lax.broadcasted_iota(jnp.int32, (docs, docs), 0)
    col = lax.broadcasted_iota(jnp.int32, (docs, docs), 1)
    lane = lax.broadcasted_iota(jnp.int32, (docs, LANES), 1)
    target = lax.broadcasted_iota(jnp.int32, (slots, docs), 0)
    load_cluster.wait()
    cluster = jnp.broadcast_to(cluster_ref[...], (docs, docs))
    cluster_col = jnp.sum(jnp.where(row == col, cluster, 0), axis=1, keepdims=True)
    earlier = (cluster_col == cluster) & (row < col)
    slot = jnp.sum(earlier.astype(jnp.int32), axis=0, keepdims=True)
    place = cluster_ref[...] * SLOTS + slot
    place_ref[...] = place
    onehot = (target == jnp.broadcast_to(place, (slots, docs))).astype(jnp.float32).astype(jnp.bfloat16)
    load_rank.wait()
    rank = jnp.broadcast_to(rank_ref[...], (docs, docs))
    age = 65536 - jnp.sum(jnp.where(row == col, rank, 0), axis=1, keepdims=True)
    high = age // 256
    low = age - high * 256
    digits = jnp.where(lane == 0, high, jnp.where(lane == 1, low, 0))
    digits = digits.astype(jnp.float32).astype(jnp.bfloat16)
    digits = jnp.dot(onehot, digits, preferred_element_type=jnp.float32).astype(jnp.bfloat16)
    send_ref[:, :, width:] = digits.reshape(clusters, SLOTS, LANES)
    load_rows.wait()
    values = rows_ref[...].astype(jnp.float32)
    total = jnp.sum(values * values, axis=1, keepdims=True)
    unit = (values / jnp.sqrt(total + EPSILON)).astype(jnp.bfloat16)
    rows = jnp.dot(onehot, unit, preferred_element_type=jnp.float32).astype(jnp.bfloat16)
    send_ref[:, :, :width] = rows.reshape(clusters, SLOTS, width)


def age_weights(shape, axis):
    place = lax.broadcasted_iota(jnp.int32, shape, axis)
    return jnp.where(place == 0, 256.0, jnp.where(place == 1, 1.0, 0.0)).astype(jnp.bfloat16)


def best_of(keys, queries_ref, width):
    contract = (((1,), (1,)), ((), ()))
    key_age = lax.dot_general(age_weights((8, LANES), 1), keys[:, width:], contract, preferred_element_type=jnp.float32)
    query_age = jnp.dot(
        queries_ref[:, width:], age_weights((LANES, LANES), 0), preferred_element_type=jnp.float32
    )
    scores = lax.dot_general(queries_ref[:, :width], keys[:, :width], contract, preferred_element_type=jnp.float32)
    allowed = key_age[:1, :] > query_age[:, :1]
    return jnp.max(jnp.where(allowed, scores, -1.0), axis=1, keepdims=True)


def make_own(width):
    def kernel(got_ref, queries_ref, best_ref):
        queries_ref[...] = got_ref[...].reshape(queries_ref.shape)
        best_ref[...] = jnp.broadcast_to(best_of(queries_ref, queries_ref, width), best_ref.shape)

    return kernel


def make_peer(width):
    def kernel(queries_ref, keys_ref, best_ref, out_ref, all_ref):
        best = best_of(keys_ref[...].reshape(queries_ref.shape), queries_ref, width)
        all_ref[...] = jnp.maximum(best_ref[...], best)
        messages = out_ref.shape[0]
        first = all_ref[pl.ds(0, messages, stride=SLOTS), :]
        second = all_ref[pl.ds(1, messages, stride=SLOTS), :]
        lane = lax.broadcasted_iota(jnp.int32, out_ref.shape, 1)
        out_ref[...] = jnp.where(lane == 0, first, second)

    return kernel


def unpack_kernel(scores_ref, place_ref, out_ref):
    clusters = scores_ref.shape[0]
    docs = place_ref.shape[1]
    place = jnp.broadcast_to(place_ref[...], (clusters, docs))
    row = lax.broadcasted_iota(jnp.int32, (clusters, docs), 0) * SLOTS
    first = jnp.where(place == row, scores_ref[:, 0:1], 0.0)
    second = jnp.where(place == row + 1, scores_ref[:, 1:2], 0.0)
    out_ref[...] = jnp.sum(first + second, axis=0, keepdims=True)


def make_per_device(docs_axis, split_axis):
    devices = docs_axis * split_axis
    clusters = devices // 2
    slots = clusters * SLOTS

    groups = [
        [d * split_axis + s for d in range(core, docs_axis, 2) for s in range(split_axis)]
        for core in range(2)
    ]
    partner = [(d, d ^ 1) for d in range(docs_axis)]
    both = ("docs", "split")

    def per_device(embeddings, cluster_id, rank):
        docs, width = embeddings.shape
        wide = width + LANES
        send, place = pl.pallas_call(
            pack_kernel,
            out_shape=(
                jax.ShapeDtypeStruct((clusters, SLOTS, wide), jnp.bfloat16),
                jax.ShapeDtypeStruct((1, docs), jnp.int32),
            ),
            in_specs=[pl.BlockSpec(memory_space=pltpu.HBM)] * 3,
            scratch_shapes=[
                pltpu.VMEM((docs, width), jnp.bfloat16),
                pltpu.VMEM((1, docs), jnp.int32),
                pltpu.VMEM((1, docs), jnp.int32),
                pltpu.SemaphoreType.DMA((3,)),
            ],
            name="pack", compiler_params=PACKED,
        )(
            pltpu.with_memory_space_constraint(embeddings, pltpu.HBM),
            pltpu.with_memory_space_constraint(cluster_id.reshape(1, docs), pltpu.HBM),
            pltpu.with_memory_space_constraint(rank.reshape(1, docs), pltpu.HBM),
        )
        got = lax.all_to_all(send, both, 0, 0, axis_index_groups=groups, tiled=True)
        keys = lax.ppermute(got, "docs", partner)
        queries, best = pl.pallas_call(
            make_own(width),
            out_shape=(
                jax.ShapeDtypeStruct((slots, wide), jnp.bfloat16),
                jax.ShapeDtypeStruct((slots, LANES), jnp.float32),
            ),
            name="own",
            compiler_params=PARAMS,
        )(got)
        scores = pl.pallas_call(
            make_peer(width),
            out_shape=jax.ShapeDtypeStruct((clusters, LANES), jnp.float32),
            scratch_shapes=[pltpu.VMEM((slots, LANES), jnp.float32)],
            name="peer", compiler_params=PACKED,
        )(queries, keys, best)
        back = lax.all_to_all(
            scores.reshape(clusters, 1, LANES), both, 0, 0, axis_index_groups=groups, tiled=True
        ).reshape(clusters, LANES)
        out = pl.pallas_call(
            unpack_kernel, out_shape=jax.ShapeDtypeStruct((1, docs), jnp.float32), name="unpack", compiler_params=PARAMS
        )(back, place)
        return out.reshape(docs)

    return per_device


def solution(mesh):
    placed = (P(("docs", "split"), None), P(("docs", "split")), P(("docs", "split")))
    per_device = make_per_device(mesh.shape["docs"], mesh.shape["split"])
    return jax.shard_map(
        per_device, mesh=mesh, in_specs=placed, out_specs=P(("docs", "split")), check_vma=False
    )
```

```python
import jax
import jax.numpy as jnp
from jax import lax
from jax.experimental import pallas as pl
from jax.experimental.pallas import tpu as pltpu
from jax.sharding import PartitionSpec as P

EPSILON = 1e-06
SLOTS = 2
LANES = 128
PARAMS = pltpu.CompilerParams(vmem_limit_bytes=16 << 20)
PACKED = pltpu.CompilerParams(vmem_limit_bytes=16 << 20)


def pack_kernel(rows_hbm, cluster_hbm, rank_hbm, send_ref, place_ref, rows_ref, cluster_ref, rank_ref, sems):
    load_cluster = pltpu.make_async_copy(cluster_hbm, cluster_ref, sems.at[0])
    load_rank = pltpu.make_async_copy(rank_hbm, rank_ref, sems.at[1])
    load_rows = pltpu.make_async_copy(rows_hbm, rows_ref, sems.at[2])
    load_cluster.start()
    load_rank.start()
    load_rows.start()
    docs, width = rows_ref.shape
    clusters = send_ref.shape[0]
    slots = clusters * SLOTS
    row = lax.broadcasted_iota(jnp.int32, (docs, docs), 0)
    col = lax.broadcasted_iota(jnp.int32, (docs, docs), 1)
    lane = lax.broadcasted_iota(jnp.int32, (docs, LANES), 1)
    target = lax.broadcasted_iota(jnp.int32, (slots, docs), 0)
    load_cluster.wait()
    cluster = jnp.broadcast_to(cluster_ref[...], (docs, docs))
    cluster_col = jnp.sum(jnp.where(row == col, cluster, 0), axis=1, keepdims=True)
    earlier = (cluster_col == cluster) & (row < col)
    slot = jnp.sum(earlier.astype(jnp.int32), axis=0, keepdims=True)
    place = cluster_ref[...] * SLOTS + slot
    place_ref[...] = place
    onehot = (target == jnp.broadcast_to(place, (slots, docs))).astype(jnp.float32).astype(jnp.bfloat16)
    load_rank.wait()
    rank = jnp.broadcast_to(rank_ref[...], (docs, docs))
    age = 65536 - jnp.sum(jnp.where(row == col, rank, 0), axis=1, keepdims=True)
    high = age // 256
    low = age - high * 256
    digits = jnp.where(lane == 0, high, jnp.where(lane == 1, low, 0))
    digits = digits.astype(jnp.float32).astype(jnp.bfloat16)
    digits = jnp.dot(onehot, digits, preferred_element_type=jnp.float32).astype(jnp.bfloat16)
    send_ref[:, :, width:] = digits.reshape(clusters, SLOTS, LANES)
    load_rows.wait()
    values = rows_ref[...].astype(jnp.float32)
    total = jnp.sum(values * values, axis=1, keepdims=True)
    unit = (values / jnp.sqrt(total + EPSILON)).astype(jnp.bfloat16)
    rows = jnp.dot(onehot, unit, preferred_element_type=jnp.float32).astype(jnp.bfloat16)
    send_ref[:, :, :width] = rows.reshape(clusters, SLOTS, width)


def age_weights(shape, axis):
    place = lax.broadcasted_iota(jnp.int32, shape, axis)
    return jnp.where(place == 0, 256.0, jnp.where(place == 1, 1.0, 0.0)).astype(jnp.bfloat16)


def best_of(keys, queries_ref, width):
    contract = (((1,), (1,)), ((), ()))
    key_age = lax.dot_general(age_weights((8, LANES), 1), keys[:, width:], contract, preferred_element_type=jnp.float32)
    query_age = jnp.dot(
        queries_ref[:, width:], age_weights((LANES, LANES), 0), preferred_element_type=jnp.float32
    )
    scores = lax.dot_general(queries_ref[:, :width], keys[:, :width], contract, preferred_element_type=jnp.float32)
    allowed = key_age[:1, :] > query_age[:, :1]
    return jnp.max(jnp.where(allowed, scores, -1.0), axis=1, keepdims=True)


def make_own(width):
    def kernel(got_ref, queries_ref, best_ref):
        queries_ref[...] = got_ref[...].reshape(queries_ref.shape)
        best_ref[...] = jnp.broadcast_to(best_of(queries_ref, queries_ref, width), best_ref.shape)

    return kernel


def make_peer(width):
    def kernel(queries_ref, keys_ref, best_ref, out_ref, all_ref):
        best = best_of(keys_ref[...].reshape(queries_ref.shape), queries_ref, width)
        all_ref[...] = jnp.maximum(best_ref[...], best)
        messages = out_ref.shape[0]
        first = all_ref[pl.ds(0, messages, stride=SLOTS), :]
        second = all_ref[pl.ds(1, messages, stride=SLOTS), :]
        lane = lax.broadcasted_iota(jnp.int32, out_ref.shape, 1)
        out_ref[...] = jnp.where(lane == 0, first, second)

    return kernel


def unpack_kernel(scores_ref, place_ref, out_ref):
    clusters = scores_ref.shape[0]
    docs = place_ref.shape[1]
    place = jnp.broadcast_to(place_ref[...], (clusters, docs))
    row = lax.broadcasted_iota(jnp.int32, (clusters, docs), 0) * SLOTS
    first = jnp.where(place == row, scores_ref[:, 0:1], 0.0)
    second = jnp.where(place == row + 1, scores_ref[:, 1:2], 0.0)
    out_ref[...] = jnp.sum(first + second, axis=0, keepdims=True)


def make_per_device(docs_axis, split_axis):
    devices = docs_axis * split_axis
    clusters = devices // 2
    slots = clusters * SLOTS

    side = round((docs_axis // 2) ** 0.5)
    groups = [
        [
            ((((diagonal + z) % side) * side + z) * 2 + core) * split_axis + x
            for diagonal in range(side)
            for z in range(side)
            for x in range(split_axis)
        ]
        for core in range(2)
    ]
    partner = [(d, d ^ 1) for d in range(docs_axis)]
    both = ("docs", "split")

    def per_device(embeddings, cluster_id, rank):
        docs, width = embeddings.shape
        wide = width + LANES
        send, place = pl.pallas_call(
            pack_kernel,
            out_shape=(
                jax.ShapeDtypeStruct((clusters, SLOTS, wide), jnp.bfloat16),
                jax.ShapeDtypeStruct((1, docs), jnp.int32),
            ),
            in_specs=[pl.BlockSpec(memory_space=pltpu.HBM)] * 3,
            scratch_shapes=[
                pltpu.VMEM((docs, width), jnp.bfloat16),
                pltpu.VMEM((1, docs), jnp.int32),
                pltpu.VMEM((1, docs), jnp.int32),
                pltpu.SemaphoreType.DMA((3,)),
            ],
            name="pack", compiler_params=PACKED,
        )(
            pltpu.with_memory_space_constraint(embeddings, pltpu.HBM),
            pltpu.with_memory_space_constraint(cluster_id.reshape(1, docs), pltpu.HBM),
            pltpu.with_memory_space_constraint(rank.reshape(1, docs), pltpu.HBM),
        )
        got = lax.all_to_all(send, both, 0, 0, axis_index_groups=groups, tiled=True)
        keys = lax.ppermute(got, "docs", partner)
        queries, best = pl.pallas_call(
            make_own(width),
            out_shape=(
                jax.ShapeDtypeStruct((slots, wide), jnp.bfloat16),
                jax.ShapeDtypeStruct((slots, LANES), jnp.float32),
            ),
            name="own",
            compiler_params=PARAMS,
        )(got)
        scores = pl.pallas_call(
            make_peer(width),
            out_shape=jax.ShapeDtypeStruct((clusters, LANES), jnp.float32),
            scratch_shapes=[pltpu.VMEM((slots, LANES), jnp.float32)],
            name="peer", compiler_params=PACKED,
        )(queries, keys, best)
        back = lax.all_to_all(
            scores.reshape(clusters, 1, LANES), both, 0, 0, axis_index_groups=groups, tiled=True
        ).reshape(clusters, LANES)
        out = pl.pallas_call(
            unpack_kernel, out_shape=jax.ShapeDtypeStruct((1, docs), jnp.float32), name="unpack", compiler_params=PARAMS
        )(back, place)
        return out.reshape(docs)

    return per_device


def solution(mesh):
    placed = (P(("docs", "split"), None), P(("docs", "split")), P(("docs", "split")))
    per_device = make_per_device(mesh.shape["docs"], mesh.shape["split"])
    return jax.shard_map(
        per_device, mesh=mesh, in_specs=placed, out_specs=P(("docs", "split")), check_vma=False
    )
```

```python
import jax
import jax.numpy as jnp
from jax import lax
from jax.experimental import pallas as pl
from jax.experimental.pallas import tpu as pltpu
from jax.sharding import PartitionSpec as P

EPSILON = 1e-06
SLOTS = 2
LANES = 128
PARAMS = pltpu.CompilerParams(vmem_limit_bytes=16 << 20)
PACKED = pltpu.CompilerParams(vmem_limit_bytes=16 << 20)


def pack_kernel(rows_hbm, cluster_hbm, rank_hbm, send_ref, place_ref, rows_ref, cluster_ref, rank_ref, sems):
    load_cluster = pltpu.make_async_copy(cluster_hbm, cluster_ref, sems.at[0])
    load_rank = pltpu.make_async_copy(rank_hbm, rank_ref, sems.at[1])
    load_rows = pltpu.make_async_copy(rows_hbm, rows_ref, sems.at[2])
    load_cluster.start()
    load_rank.start()
    load_rows.start()
    docs, width = rows_ref.shape
    clusters = send_ref.shape[0]
    slots = clusters * SLOTS
    row = lax.broadcasted_iota(jnp.int32, (docs, docs), 0)
    col = lax.broadcasted_iota(jnp.int32, (docs, docs), 1)
    lane = lax.broadcasted_iota(jnp.int32, (docs, LANES), 1)
    target = lax.broadcasted_iota(jnp.int32, (slots, docs), 0)
    load_cluster.wait()
    cluster = jnp.broadcast_to(cluster_ref[...], (docs, docs))
    cluster_col = jnp.sum(jnp.where(row == col, cluster, 0), axis=1, keepdims=True)
    earlier = (cluster_col == cluster) & (row < col)
    slot = jnp.sum(earlier.astype(jnp.int32), axis=0, keepdims=True)
    place = cluster_ref[...] * SLOTS + slot
    place_ref[...] = place
    onehot = (target == jnp.broadcast_to(place, (slots, docs))).astype(jnp.float32).astype(jnp.bfloat16)
    load_rank.wait()
    rank = jnp.broadcast_to(rank_ref[...], (docs, docs))
    age = 65536 - jnp.sum(jnp.where(row == col, rank, 0), axis=1, keepdims=True)
    high = age // 256
    low = age - high * 256
    digits = jnp.where(lane == 0, high, jnp.where(lane == 1, low, 0))
    digits = digits.astype(jnp.float32).astype(jnp.bfloat16)
    digits = jnp.dot(onehot, digits, preferred_element_type=jnp.float32).astype(jnp.bfloat16)
    send_ref[:, :, width:] = digits.reshape(clusters, SLOTS, LANES)
    load_rows.wait()
    values = rows_ref[...].astype(jnp.float32)
    total = jnp.sum(values * values, axis=1, keepdims=True)
    unit = (values / jnp.sqrt(total + EPSILON)).astype(jnp.bfloat16)
    rows = jnp.dot(onehot, unit, preferred_element_type=jnp.float32).astype(jnp.bfloat16)
    send_ref[:, :, :width] = rows.reshape(clusters, SLOTS, width)


def age_weights(shape, axis):
    place = lax.broadcasted_iota(jnp.int32, shape, axis)
    return jnp.where(place == 0, 256.0, jnp.where(place == 1, 1.0, 0.0)).astype(jnp.bfloat16)


def best_of(keys, queries_ref, width):
    contract = (((1,), (1,)), ((), ()))
    key_age = lax.dot_general(age_weights((8, LANES), 1), keys[:, width:], contract, preferred_element_type=jnp.float32)
    query_age = jnp.dot(
        queries_ref[:, width:], age_weights((LANES, LANES), 0), preferred_element_type=jnp.float32
    )
    scores = lax.dot_general(queries_ref[:, :width], keys[:, :width], contract, preferred_element_type=jnp.float32)
    allowed = key_age[:1, :] > query_age[:, :1]
    return jnp.max(jnp.where(allowed, scores, -1.0), axis=1, keepdims=True)


def make_own(width):
    def kernel(got_ref, queries_ref, best_ref):
        queries_ref[...] = got_ref[...].reshape(queries_ref.shape)
        best_ref[...] = jnp.broadcast_to(best_of(queries_ref, queries_ref, width), best_ref.shape)

    return kernel


def make_peer(width):
    def kernel(queries_ref, keys_ref, best_ref, out_ref, all_ref):
        best = best_of(keys_ref[...].reshape(queries_ref.shape), queries_ref, width)
        all_ref[...] = jnp.maximum(best_ref[...], best)
        messages = out_ref.shape[0]
        first = all_ref[pl.ds(0, messages, stride=SLOTS), :]
        second = all_ref[pl.ds(1, messages, stride=SLOTS), :]
        lane = lax.broadcasted_iota(jnp.int32, out_ref.shape, 1)
        out_ref[...] = jnp.where(lane == 0, first, second)

    return kernel


def unpack_kernel(scores_ref, place_ref, out_ref):
    clusters = scores_ref.shape[0]
    docs = place_ref.shape[1]
    place = jnp.broadcast_to(place_ref[...], (clusters, docs))
    row = lax.broadcasted_iota(jnp.int32, (clusters, docs), 0) * SLOTS
    first = jnp.where(place == row, scores_ref[:, 0:1], 0.0)
    second = jnp.where(place == row + 1, scores_ref[:, 1:2], 0.0)
    out_ref[...] = jnp.sum(first + second, axis=0, keepdims=True)


def make_per_device(docs_axis, split_axis):
    devices = docs_axis * split_axis
    clusters = devices // 2
    slots = clusters * SLOTS

    side = round((docs_axis // 2) ** 0.5)
    groups = [
        [
            ((y * side + z) * 2 + (x + y + z + member) % 2) * split_axis + x
            for y in range(side)
            for z in range(side)
            for x in range(split_axis)
        ]
        for member in range(2)
    ]
    partner = [(d, d ^ 1) for d in range(docs_axis)]
    both = ("docs", "split")

    def per_device(embeddings, cluster_id, rank):
        docs, width = embeddings.shape
        wide = width + LANES
        send, place = pl.pallas_call(
            pack_kernel,
            out_shape=(
                jax.ShapeDtypeStruct((clusters, SLOTS, wide), jnp.bfloat16),
                jax.ShapeDtypeStruct((1, docs), jnp.int32),
            ),
            in_specs=[pl.BlockSpec(memory_space=pltpu.HBM)] * 3,
            scratch_shapes=[
                pltpu.VMEM((docs, width), jnp.bfloat16),
                pltpu.VMEM((1, docs), jnp.int32),
                pltpu.VMEM((1, docs), jnp.int32),
                pltpu.SemaphoreType.DMA((3,)),
            ],
            name="pack", compiler_params=PACKED,
        )(
            pltpu.with_memory_space_constraint(embeddings, pltpu.HBM),
            pltpu.with_memory_space_constraint(cluster_id.reshape(1, docs), pltpu.HBM),
            pltpu.with_memory_space_constraint(rank.reshape(1, docs), pltpu.HBM),
        )
        got = lax.all_to_all(send, both, 0, 0, axis_index_groups=groups, tiled=True)
        keys = lax.ppermute(got, "docs", partner)
        queries, best = pl.pallas_call(
            make_own(width),
            out_shape=(
                jax.ShapeDtypeStruct((slots, wide), jnp.bfloat16),
                jax.ShapeDtypeStruct((slots, LANES), jnp.float32),
            ),
            name="own",
            compiler_params=PARAMS,
        )(got)
        scores = pl.pallas_call(
            make_peer(width),
            out_shape=jax.ShapeDtypeStruct((clusters, LANES), jnp.float32),
            scratch_shapes=[pltpu.VMEM((slots, LANES), jnp.float32)],
            name="peer", compiler_params=PACKED,
        )(queries, keys, best)
        back = lax.all_to_all(
            scores.reshape(clusters, 1, LANES), both, 0, 0, axis_index_groups=groups, tiled=True
        ).reshape(clusters, LANES)
        out = pl.pallas_call(
            unpack_kernel, out_shape=jax.ShapeDtypeStruct((1, docs), jnp.float32), name="unpack", compiler_params=PARAMS
        )(back, place)
        return out.reshape(docs)

    return per_device


def solution(mesh):
    placed = (P(("docs", "split"), None), P(("docs", "split")), P(("docs", "split")))
    per_device = make_per_device(mesh.shape["docs"], mesh.shape["split"])
    return jax.shard_map(
        per_device, mesh=mesh, in_specs=placed, out_specs=P(("docs", "split")), check_vma=False
    )
```

```python
import jax
import jax.numpy as jnp
from jax import lax
from jax.experimental import pallas as pl
from jax.experimental.pallas import tpu as pltpu
from jax.sharding import PartitionSpec as P

EPSILON = 1e-06
SLOTS = 2
LANES = 128
PARAMS = pltpu.CompilerParams(vmem_limit_bytes=16 << 20)
PACKED = pltpu.CompilerParams(vmem_limit_bytes=16 << 20)


def pack_kernel(rows_hbm, cluster_hbm, rank_hbm, send_ref, place_ref, rows_ref, cluster_ref, rank_ref, sems):
    load_cluster = pltpu.make_async_copy(cluster_hbm, cluster_ref, sems.at[0])
    load_rank = pltpu.make_async_copy(rank_hbm, rank_ref, sems.at[1])
    load_rows = pltpu.make_async_copy(rows_hbm, rows_ref, sems.at[2])
    load_cluster.start()
    load_rank.start()
    load_rows.start()
    docs, width = rows_ref.shape
    clusters = send_ref.shape[0]
    slots = clusters * SLOTS
    row = lax.broadcasted_iota(jnp.int32, (docs, docs), 0)
    col = lax.broadcasted_iota(jnp.int32, (docs, docs), 1)
    lane = lax.broadcasted_iota(jnp.int32, (docs, LANES), 1)
    target = lax.broadcasted_iota(jnp.int32, (slots, docs), 0)
    load_cluster.wait()
    cluster = jnp.broadcast_to(cluster_ref[...], (docs, docs))
    cluster_col = jnp.sum(jnp.where(row == col, cluster, 0), axis=1, keepdims=True)
    earlier = (cluster_col == cluster) & (row < col)
    slot = jnp.sum(earlier.astype(jnp.int32), axis=0, keepdims=True)
    place = cluster_ref[...] * SLOTS + slot
    place_ref[...] = place
    onehot = jnp.where(target == place, 1.0, 0.0).astype(jnp.bfloat16)
    load_rank.wait()
    rank = jnp.broadcast_to(rank_ref[...], (docs, docs))
    age = 65536 - jnp.sum(jnp.where(row == col, rank, 0), axis=1, keepdims=True)
    high = age >> 8
    low = age & 255
    digits = jnp.where(lane == 0, high, jnp.where(lane == 1, low, 0))
    digits = digits.astype(jnp.float32).astype(jnp.bfloat16)
    digits = jnp.dot(onehot, digits, preferred_element_type=jnp.float32).astype(jnp.bfloat16)
    send_ref[:, :, width:] = digits.reshape(clusters, SLOTS, LANES)
    load_rows.wait()
    values = rows_ref[...].astype(jnp.float32)
    total = jnp.sum(values * values, axis=1, keepdims=True)
    unit = (values / jnp.sqrt(total + EPSILON)).astype(jnp.bfloat16)
    rows = jnp.dot(onehot, unit, preferred_element_type=jnp.float32).astype(jnp.bfloat16)
    send_ref[:, :, :width] = rows.reshape(clusters, SLOTS, width)


def age_weights(shape, axis):
    place = lax.broadcasted_iota(jnp.int32, shape, axis)
    return jnp.where(place == 0, 256.0, jnp.where(place == 1, 1.0, 0.0)).astype(jnp.bfloat16)


def best_of(keys, queries_ref, width):
    contract = (((1,), (1,)), ((), ()))
    key_age = lax.dot_general(age_weights((8, LANES), 1), keys[:, width:], contract, preferred_element_type=jnp.float32)
    query_age = jnp.dot(
        queries_ref[:, width:], age_weights((LANES, LANES), 0), preferred_element_type=jnp.float32
    )
    scores = lax.dot_general(queries_ref[:, :width], keys[:, :width], contract, preferred_element_type=jnp.float32)
    allowed = key_age[:1, :] > query_age[:, :1]
    return jnp.max(jnp.where(allowed, scores, -1.0), axis=1, keepdims=True)


def make_own(width):
    def kernel(got_ref, queries_ref, best_ref):
        queries_ref[...] = got_ref[...].reshape(queries_ref.shape)
        best_ref[...] = jnp.broadcast_to(best_of(queries_ref, queries_ref, width), best_ref.shape)

    return kernel


def make_peer(width):
    def kernel(queries_ref, keys_ref, best_ref, out_ref, all_ref):
        best = best_of(keys_ref[...].reshape(queries_ref.shape), queries_ref, width)
        all_ref[...] = jnp.maximum(best_ref[...], best)
        messages = out_ref.shape[0]
        first = all_ref[pl.ds(0, messages, stride=SLOTS), :]
        second = all_ref[pl.ds(1, messages, stride=SLOTS), :]
        lane = lax.broadcasted_iota(jnp.int32, out_ref.shape, 1)
        out_ref[...] = jnp.where(lane == 0, first, second)

    return kernel


def unpack_kernel(scores_ref, place_ref, out_ref):
    clusters = scores_ref.shape[0]
    docs = place_ref.shape[1]
    place = jnp.broadcast_to(place_ref[...], (clusters, docs))
    row = lax.broadcasted_iota(jnp.int32, (clusters, docs), 0) * SLOTS
    first = jnp.where(place == row, scores_ref[:, 0:1], 0.0)
    second = jnp.where(place == row + 1, scores_ref[:, 1:2], 0.0)
    out_ref[...] = jnp.sum(first + second, axis=0, keepdims=True)


def make_per_device(docs_axis, split_axis):
    devices = docs_axis * split_axis
    clusters = devices // 2
    slots = clusters * SLOTS

    groups = [
        [d * split_axis + s for d in range(core, docs_axis, 2) for s in range(split_axis)]
        for core in range(2)
    ]
    partner = [(d, d ^ 1) for d in range(docs_axis)]
    both = ("docs", "split")

    def per_device(embeddings, cluster_id, rank):
        docs, width = embeddings.shape
        wide = width + LANES
        send, place = pl.pallas_call(
            pack_kernel,
            out_shape=(
                jax.ShapeDtypeStruct((clusters, SLOTS, wide), jnp.bfloat16),
                jax.ShapeDtypeStruct((1, docs), jnp.int32),
            ),
            in_specs=[pl.BlockSpec(memory_space=pltpu.HBM)] * 3,
            scratch_shapes=[
                pltpu.VMEM((docs, width), jnp.bfloat16),
                pltpu.VMEM((1, docs), jnp.int32),
                pltpu.VMEM((1, docs), jnp.int32),
                pltpu.SemaphoreType.DMA((3,)),
            ],
            name="pack", compiler_params=PACKED,
        )(
            pltpu.with_memory_space_constraint(embeddings, pltpu.HBM),
            pltpu.with_memory_space_constraint(cluster_id.reshape(1, docs), pltpu.HBM),
            pltpu.with_memory_space_constraint(rank.reshape(1, docs), pltpu.HBM),
        )
        got = lax.all_to_all(send, both, 0, 0, axis_index_groups=groups, tiled=True)
        keys = lax.ppermute(got, "docs", partner)
        queries, best = pl.pallas_call(
            make_own(width),
            out_shape=(
                jax.ShapeDtypeStruct((slots, wide), jnp.bfloat16),
                jax.ShapeDtypeStruct((slots, LANES), jnp.float32),
            ),
            name="own",
            compiler_params=PARAMS,
        )(got)
        scores = pl.pallas_call(
            make_peer(width),
            out_shape=jax.ShapeDtypeStruct((clusters, LANES), jnp.float32),
            scratch_shapes=[pltpu.VMEM((slots, LANES), jnp.float32)],
            name="peer", compiler_params=PACKED,
        )(queries, keys, best)
        back = lax.all_to_all(
            scores.reshape(clusters, 1, LANES), both, 0, 0, axis_index_groups=groups, tiled=True
        ).reshape(clusters, LANES)
        out = pl.pallas_call(
            unpack_kernel, out_shape=jax.ShapeDtypeStruct((1, docs), jnp.float32), name="unpack", compiler_params=PARAMS
        )(back, place)
        return out.reshape(docs)

    return per_device


def solution(mesh):
    placed = (P(("docs", "split"), None), P(("docs", "split")), P(("docs", "split")))
    per_device = make_per_device(mesh.shape["docs"], mesh.shape["split"])
    return jax.shard_map(
        per_device, mesh=mesh, in_specs=placed, out_specs=P(("docs", "split")), check_vma=False
    )
```
